512 devices in a mesh: row: 32 (over x_hi, z, core), col: 16 (over y, x_lo).
Axes of the slice: x: 4 (x_hi: 2, x_lo: 2; x = x_hi * 2 + x_lo), y: 8, z: 8, core: 2. Of those that a mesh axis runs over, the one named last changes fastest.
Arguments:
- inputs: bfloat16 [256, 8192], P('col', 'row'), may hold values from -6 to 6
- w_up: bfloat16 [8192, 26624], P('row', 'col'), may hold values from -0.0625 to 0.0625
- w_down: bfloat16 [26624, 8192], P('col', 'row'), may hold values from -0.0390625 to 0.0390625
- out_grad: bfloat16 [256, 8192], P('col', 'row'), may hold values from -6 to 6
Outputs:
- result: bfloat16 [256, 8192], P('col', 'row')
- in_grad: bfloat16 [256, 8192], P('col', 'row')
- up_grad: bfloat16 [8192, 26624], P('row', 'col')
- down_grad: bfloat16 [26624, 8192], P('col', 'row')
The draws below stay inside these ranges and needn't reach their ends.
All inputs are finite; a program needn't handle non-finite values.
Results may differ from the reference program's by a relative error of at most 0.005.
Values may be sent and summed in bfloat16 or wider, within the bound.
No kernel may reach another device: no remote copies, remote signals or barrier semaphores. Data moves between devices by JAX's collectives and lax.ppermute only.
A program may use at most 64 MiB of HBM per device.

```python
import jax
import jax.numpy as jnp

D = 8192
FF = 26624
TOKENS = 256


def steps_of(own_key, dims, shards, low, high):
    loudness, own = 1.0, jax.random.fold_in(own_key, 6)
    for dim, parts in shards:
        draws = jnp.exp(jax.random.uniform(jax.random.fold_in(own, dim), (parts,), jnp.float32, low / len(shards), high / len(shards)))
        loudness = loudness * jnp.repeat(draws, dims[dim] // parts).reshape([-1 if axis == dim else 1 for axis in range(len(dims))])
    return loudness


def normal_values(rng, extent, spread, bound, split=(), kind=jnp.bfloat16):
    loudness = steps_of(rng, extent, split, -0.22, 0.18) if split else 1.0
    values = jax.random.normal(rng, extent, jnp.float32) * spread * loudness
    return jnp.minimum(jnp.maximum(values, -bound), bound).astype(kind)


def setup_inputs(seed: int = 0) -> dict:
    splits = jax.random.split(jax.random.key(seed), 5)
    inputs = normal_values(splits[0], (TOKENS, D), 1.0, 6.0, ((0, 16), (1, 32)))
    w_up = normal_values(splits[1], (D, FF), D ** -0.5, 0.0625, ((0, 32), (1, 16)))
    w_down = normal_values(splits[2], (FF, D), FF ** -0.5, 0.0390625, ((0, 16), (1, 32)))
    out_grad = normal_values(splits[3], (TOKENS, D), 1.0, 6.0, ((0, 16), (1, 32)))
    return {"inputs": inputs, "w_up": w_up, "w_down": w_down, "out_grad": out_grad}


def gelu_value(hidden):
    return 0.5 * hidden * (1.0 + jax.scipy.special.erf(hidden * 0.7071067811865476))


def gelu_slope(hidden):
    return 0.5 * (1.0 + jax.scipy.special.erf(hidden * 0.7071067811865476)) + hidden * jnp.exp(-0.5 * hidden * hidden) * 0.3989422804014327


def reference(inputs, w_up, w_down, out_grad):
    hidden = jnp.dot(inputs, w_up, preferred_element_type=jnp.float32)
    activated = gelu_value(hidden).astype(jnp.bfloat16)
    result = jnp.dot(activated, w_down, preferred_element_type=jnp.float32).astype(jnp.bfloat16)
    act_grad = jnp.dot(out_grad, w_down.T, preferred_element_type=jnp.float32)
    hid_grad = (act_grad * gelu_slope(hidden)).astype(jnp.bfloat16)
    in_grad = jnp.dot(hid_grad, w_up.T, preferred_element_type=jnp.float32).astype(jnp.bfloat16)
    up_grad = jnp.dot(inputs.T, hid_grad, preferred_element_type=jnp.float32).astype(jnp.bfloat16)
    down_grad = jnp.dot(activated.T, out_grad, preferred_element_type=jnp.float32).astype(jnp.bfloat16)
    return (result, in_grad, up_grad, down_grad)
```

```python
import functools

import jax
import jax.numpy as jnp
from jax import lax
from jax.experimental import pallas as pl
from jax.experimental.pallas import tpu as pltpu
from jax.sharding import Mesh
from jax.sharding import PartitionSpec as P

FINE = ("x_hi", "z", "core", "y", "x_lo")
SIZES = (2, 8, 2, 8, 2)
ROW = ("x_hi", "z", "core")
CHIPS = ("x_hi", "z")
COL = ("y", "x_lo")
BF16 = jnp.bfloat16
F32 = jnp.float32
VMEM_LIMIT = 60 * 1024 * 1024


def call(kernel, out_shape, n_in, scalar=False):
    specs = [pl.BlockSpec(memory_space=pltpu.VMEM)] * n_in
    if scalar:
        specs = [pl.BlockSpec(memory_space=pltpu.SMEM)] + specs
    out_specs = jax.tree.map(lambda _: pl.BlockSpec(memory_space=pltpu.VMEM), out_shape)
    run = pl.pallas_call(
        kernel,
        out_shape=out_shape,
        in_specs=specs,
        out_specs=out_specs,
        compiler_params=pltpu.CompilerParams(vmem_limit_bytes=VMEM_LIMIT),
    )

    def placed(*args):
        head, rest = args[: len(args) - n_in], args[len(args) - n_in :]
        return run(*head, *(pltpu.with_memory_space_constraint(a, pltpu.VMEM) for a in rest))

    return placed


def dot_nn(a, b):
    return jnp.dot(a, b, preferred_element_type=F32)


def dot_nt(a, b):
    return lax.dot_general(a, b, (((1,), (1,)), ((), ())), preferred_element_type=F32)


def dot_tn(a, b):
    return lax.dot_general(a, b, (((0,), (0,)), ((), ())), preferred_element_type=F32)


def up_kernel(which_ref, g_ref, w_up_ref, w_down_ref, out_ref):
    half, groups, feats = g_ref.shape[0] // 2, out_ref.shape[0], out_ref.shape[3]
    rows = g_ref[pl.ds(which_ref[0] * half, half)]
    x = rows[:, 0].reshape(-1, rows.shape[-1])
    c = rows[:, 1].reshape(-1, rows.shape[-1])
    out_ref[:, 0] = dot_nn(x, w_up_ref[...]).astype(out_ref.dtype).reshape(groups, -1, feats)
    out_ref[:, 1] = dot_nt(c, w_down_ref[...]).astype(out_ref.dtype).reshape(groups, -1, feats)


def middle_kernel(x_ref, out_ref):
    total = jnp.sum(x_ref[...].astype(F32), axis=0)
    hidden, act_grad = total[0], total[1]
    cdf = 0.5 * (1.0 + lax.erf(hidden * 0.7071067811865476))
    slope = cdf + hidden * jnp.exp(-0.5 * hidden * hidden) * 0.3989422804014327
    activated = (hidden * cdf).astype(BF16)
    hid_grad = (act_grad * slope).astype(BF16)
    for i in range(out_ref.shape[0]):
        out_ref[i, 0] = activated
        out_ref[i, 1] = hid_grad


def down_kernel(h_ref, w_up_ref, w_down_ref, out_ref):
    feats = h_ref.shape[-1]
    a = h_ref[:, 0].reshape(-1, feats)
    d = h_ref[:, 1].reshape(-1, feats)
    shape = (out_ref.shape[0],) + out_ref.shape[2:]
    out_ref[:, 0] = dot_nn(a, w_down_ref[...]).astype(BF16).reshape(shape)
    out_ref[:, 1] = dot_nt(d, w_up_ref[...]).astype(BF16).reshape(shape)


def grad_kernel(core_ref, g_ref, own_ref, other_ref, up_ref, down_ref):
    half, feats = g_ref.shape[0] // 2, own_ref.shape[-1]
    core = core_ref[0]
    up, down = 0.0, 0.0
    for ref, which in ((own_ref, core), (other_ref, 1 - core)):
        rows = g_ref[pl.ds(which * half, half)]
        x = rows[:, 0].reshape(-1, rows.shape[-1])
        c = rows[:, 1].reshape(-1, rows.shape[-1])
        a = ref[:, 0].reshape(-1, feats)
        d = ref[:, 1].reshape(-1, feats)
        up = up + dot_tn(x, d)
        down = down + dot_tn(a, c)
    up_ref[...] = up.astype(BF16)
    down_ref[...] = down.astype(BF16)


def on_device(inputs, w_up, w_down, out_grad):
    n_col, n_chips = 16, 16
    tok, model = inputs.shape
    feats = w_up.shape[1]
    half = tok * n_col // 2
    sub = half // n_chips
    core = lax.axis_index("core").astype(jnp.int32)
    core_own, core_other = core.reshape(1), (1 - core).reshape(1)
    swap = [(0, 1), (1, 0)]

    both = jnp.stack([inputs, out_grad])
    g = lax.all_to_all(
        jnp.broadcast_to(both[None], (n_col,) + both.shape), COL, 0, 0, tiled=True
    )
    hid = (n_chips, 2, sub, feats)
    up16 = call(up_kernel, pltpu.VMEM(hid, BF16), 3, True)
    up32 = call(up_kernel, pltpu.VMEM(hid, F32), 3, True)
    sent = lax.ppermute(up16(core_other, g, w_up, w_down), "core", swap)
    part = (up32(core_own, g, w_up, w_down) + sent.astype(F32)).astype(BF16)
    part = lax.all_to_all(part, CHIPS, 0, 0, tiled=True)
    mine = call(middle_kernel, pltpu.VMEM(hid, BF16), 1)(part)
    own = lax.all_to_all(mine, CHIPS, 0, 0, tiled=True)
    other = lax.ppermute(own, "core", swap)
    down = call(down_kernel, pltpu.VMEM((n_col // 2, 2, tok, model), BF16), 3)
    out_own = down(own, w_up, w_down)
    out_other = down(other, w_up, w_down)
    first = jnp.where(core == 0, out_own, out_other)
    second = jnp.where(core == 0, out_other, out_own)
    outs = lax.all_to_all(jnp.concatenate([first, second]), COL, 0, 0, tiled=True)
    up_grad, down_grad = call(
        grad_kernel,
        (jax.ShapeDtypeStruct(w_up.shape, BF16), jax.ShapeDtypeStruct(w_down.shape, BF16)),
        3,
        True,
    )(core_own, g, own, other)
    outs = jnp.sum(outs.astype(F32), axis=0).astype(BF16)
    return (outs[0], outs[1], up_grad, down_grad)


def solution(mesh):
    fine = Mesh(mesh.devices.reshape(SIZES), FINE)
    return jax.shard_map(
        on_device,
        mesh=fine,
        in_specs=(P(COL, ROW), P(ROW, COL), P(COL, ROW), P(COL, ROW)),
        out_specs=(P(COL, ROW), P(COL, ROW), P(ROW, COL), P(COL, ROW)),
        check_vma=False,
    )
```

```python
import functools

import jax
import jax.numpy as jnp
from jax import lax
from jax.experimental import pallas as pl
from jax.experimental.pallas import tpu as pltpu
from jax.sharding import Mesh
from jax.sharding import PartitionSpec as P

FINE = ("x_hi", "z", "core", "y", "x_lo")
SIZES = (2, 8, 2, 8, 2)
ROW = ("x_hi", "z", "core")
CHIPS = ("x_hi", "z")
COL = ("y", "x_lo")
SWAP = [(0, 1), (1, 0)]
BF16 = jnp.bfloat16
F32 = jnp.float32
VMEM_LIMIT = 16 * 1024 * 1024


def call(kernel, outs, spaces, *args, scratch=()):
    kinds = {"s": pltpu.SMEM, "v": pltpu.VMEM, "h": pltpu.HBM, "o": pltpu.VMEM}
    ins, places = spaces[: len(args)], spaces[len(args) :]
    args = [a if s == "s" else pltpu.with_memory_space_constraint(a, kinds[s]) for a, s in zip(args, ins)]
    return pl.pallas_call(
        kernel,
        out_shape=[(jax.ShapeDtypeStruct if s == "o" else kinds[s])(*out) for s, out in zip(places, outs)],
        in_specs=[pl.BlockSpec(memory_space=kinds[s]) for s in ins],
        out_specs=[pl.BlockSpec(memory_space=kinds[s]) for s in places],
        scratch_shapes=list(scratch),
        compiler_params=pltpu.CompilerParams(vmem_limit_bytes=VMEM_LIMIT),
    )(*args)


def dot_nn(a, b):
    return jnp.dot(a, b, preferred_element_type=F32)


def dot_nt(a, b):
    return lax.dot_general(a, b, (((1,), (1,)), ((), ())), preferred_element_type=F32)


def dot_tn(a, b):
    return lax.dot_general(a, b, (((0,), (0,)), ((), ())), preferred_element_type=F32)


def flat(x):
    return x.reshape(-1, x.shape[-1])


def run_copies(pairs, sems):
    copies = [pltpu.make_async_copy(src, dst, sems.at[i]) for i, (src, dst) in enumerate(pairs)]
    for copy in copies:
        copy.start()
    return copies


def start_kernel(core_ref, x_ref, c_ref, up_in, down_in, out_ref, up_out, down_out, token, sems):
    del core_ref
    pairs = [(x_ref, token.at[0]), (c_ref, token.at[1]), (up_in, up_out), (down_in, down_out)]
    copies = run_copies(pairs, sems)
    copies[0].wait()
    copies[1].wait()
    for i in range(out_ref.shape[0]):
        out_ref[i] = token[...]
    copies[2].wait()
    copies[3].wait()


def partial_up(g_ref, which, up_ref, down_ref, out_ref):
    half = g_ref.shape[0] // 2
    rows = g_ref[pl.ds(which * half, half)]
    shape = (out_ref.shape[0],) + out_ref.shape[2:]
    out_ref[:, 0] = dot_nn(flat(rows[:, 0]), up_ref[...]).astype(out_ref.dtype).reshape(shape)
    out_ref[:, 1] = dot_nt(flat(rows[:, 1]), down_ref[...]).astype(out_ref.dtype).reshape(shape)


def up_other_kernel(core_ref, g_ref, up_ref, down_ref, out_ref):
    partial_up(g_ref, 1 - core_ref[0], up_ref, down_ref, out_ref)


def up_own_kernel(core_ref, g_ref, up_ref, down_ref, out_ref, x_ref, c_ref):
    partial_up(g_ref, core_ref[0], up_ref, down_ref, out_ref)
    x_ref[...] = flat(g_ref[:, 0]).T
    c_ref[...] = flat(g_ref[:, 1]).T


def add_kernel(a_ref, b_ref, out_ref):
    out_ref[...] = (a_ref[...] + b_ref[...].astype(F32)).astype(BF16)


def middle_kernel(x_ref, out_ref):
    total = jnp.sum(x_ref[...].astype(F32), axis=0)
    hidden, act_grad = total[0], total[1]
    cdf = 0.5 * (1.0 + lax.erf(hidden * 0.7071067811865476))
    slope = cdf + hidden * jnp.exp(-0.5 * hidden * hidden) * 0.3989422804014327
    activated = (hidden * cdf).astype(BF16)
    hid_grad = (act_grad * slope).astype(BF16)
    for i in range(out_ref.shape[0]):
        out_ref[i, 0] = activated
        out_ref[i, 1] = hid_grad


def partial_down(h_ref, up_ref, down_ref, out_ref):
    shape = (out_ref.shape[0],) + out_ref.shape[2:]
    out_ref[:, 0] = dot_nn(flat(h_ref[:, 0]), down_ref[...]).astype(BF16).reshape(shape)
    out_ref[:, 1] = dot_nt(flat(h_ref[:, 1]), up_ref[...]).astype(BF16).reshape(shape)


def down_own_kernel(h_ref, up_in, down_in, out_ref, up_out, down_out, sems):
    for copy in run_copies([(up_in, up_out), (down_in, down_out)], sems):
        copy.wait()
    partial_down(h_ref, up_out, down_out, out_ref)


def down_other_kernel(core_ref, h_ref, own_ref, up_ref, down_ref, out_ref, mine, sems):
    half = own_ref.shape[0]
    core = core_ref[0]
    first = pltpu.make_async_copy(own_ref, out_ref.at[pl.ds(core * half, half)], sems.at[0])
    first.start()
    partial_down(h_ref, up_ref, down_ref, mine)
    second = pltpu.make_async_copy(mine, out_ref.at[pl.ds((1 - core) * half, half)], sems.at[1])
    second.start()
    first.wait()
    second.wait()


def grad_kernel(core_ref, x_ref, c_ref, own_ref, other_ref, up_ref, down_ref):
    half = x_ref.shape[1] // 2
    core = core_ref[0]
    up, down = 0.0, 0.0
    for ref, which in ((own_ref, core), (other_ref, 1 - core)):
        cols = pl.ds(pl.multiple_of(which * half, half), half)
        up = up + dot_nn(x_ref[:, cols], flat(ref[:, 1]))
        down = down + dot_nn(c_ref[:, cols], flat(ref[:, 0]))
    up_ref[...] = up.astype(BF16)
    down_ref[...] = down.astype(BF16).T


def sum_kernel(x_ref, result_ref, in_grad_ref):
    total = jnp.sum(x_ref[...].astype(F32), axis=0)
    result_ref[...] = total[0].astype(BF16)
    in_grad_ref[...] = total[1].astype(BF16)


def on_device(inputs, w_up, w_down, out_grad):
    n_col, n_chips = 16, 16
    tok, model = inputs.shape
    feats = w_up.shape[1]
    half = n_col // 2
    sub = half * tok // n_chips
    core = lax.axis_index("core").astype(jnp.int32).reshape(1)
    hid = (n_chips, 2, sub, feats)
    io = (n_col, 2, tok, model)
    half_io = (half, 2, tok, model)
    turned = (model, n_col * tok)
    weights = [(w_up.shape, BF16), (w_down.shape, BF16)]
    dma = pltpu.SemaphoreType.DMA

    spread, up, down = call(
        start_kernel,
        [(io, BF16)] + weights,
        "shhhhvvv",
        core,
        inputs,
        out_grad,
        w_up,
        w_down,
        scratch=[pltpu.VMEM(io[1:], BF16), dma((4,))],
    )
    g = lax.all_to_all(spread, COL, 0, 0, tiled=True)
    (sent,) = call(up_other_kernel, [(hid, BF16)], "svvvv", core, g, up, down)
    got = lax.ppermute(sent, "core", SWAP)
    kept, x_t, c_t = call(
        up_own_kernel, [(hid, F32), (turned, BF16), (turned, BF16)], "svvvvvv", core, g, up, down
    )
    (part,) = call(add_kernel, [(hid, BF16)], "vvv", kept, got)
    part = lax.all_to_all(part, CHIPS, 0, 0, tiled=True)
    (mine,) = call(middle_kernel, [(hid, BF16)], "vv", part)
    own = lax.all_to_all(mine, CHIPS, 0, 0, tiled=True)
    other = lax.ppermute(own, "core", SWAP)
    own_out, up, down = call(
        down_own_kernel, [(half_io, BF16)] + weights, "vhhvvv", own, w_up, w_down, scratch=[dma((2,))]
    )
    (outs,) = call(
        down_other_kernel,
        [(io, BF16)],
        "svvvvh",
        core,
        other,
        own_out,
        up,
        down,
        scratch=[pltpu.VMEM(half_io, BF16), dma((2,))],
    )
    outs = lax.all_to_all(outs, COL, 0, 0, tiled=True)
    up_grad, down_grad = call(grad_kernel, weights, "svvvvoo", core, x_t, c_t, own, other)
    up_grad, down_grad, outs = lax.optimization_barrier((up_grad, down_grad, outs))
    result, in_grad = call(sum_kernel, [(inputs.shape, BF16)] * 2, "voo", outs)
    return (result, in_grad, up_grad, down_grad)


def solution(mesh):
    fine = Mesh(mesh.devices.reshape(SIZES), FINE)
    return jax.shard_map(
        on_device,
        mesh=fine,
        in_specs=(P(COL, ROW), P(ROW, COL), P(COL, ROW), P(COL, ROW)),
        out_specs=(P(COL, ROW), P(COL, ROW), P(ROW, COL), P(COL, ROW)),
        check_vma=False,
    )
```

```python
import functools

import jax
import jax.numpy as jnp
from jax import lax
from jax.experimental import pallas as pl
from jax.experimental.pallas import tpu as pltpu
from jax.sharding import Mesh
from jax.sharding import PartitionSpec as P

FINE = ("x_hi", "z", "core", "y", "x_lo")
SIZES = (2, 8, 2, 8, 2)
ROW = ("x_hi", "z", "core")
CHIPS = ("x_hi", "z")
COL = ("y", "x_lo")
SWAP = [(0, 1), (1, 0)]
COL_FIRST = 11
CHIPS_FIRST = 13
BF16 = jnp.bfloat16
F32 = jnp.float32
VMEM_LIMIT = 16 * 1024 * 1024


def call(kernel, outs, spaces, *args, scratch=()):
    kinds = {"s": pltpu.SMEM, "v": pltpu.VMEM, "h": pltpu.HBM, "o": pltpu.VMEM}
    ins, places = spaces[: len(args)], spaces[len(args) :]
    args = [a if s == "s" else pltpu.with_memory_space_constraint(a, kinds[s]) for a, s in zip(args, ins)]
    return pl.pallas_call(
        kernel,
        out_shape=[(jax.ShapeDtypeStruct if s == "o" else kinds[s])(*out) for s, out in zip(places, outs)],
        in_specs=[pl.BlockSpec(memory_space=kinds[s]) for s in ins],
        out_specs=[pl.BlockSpec(memory_space=kinds[s]) for s in places],
        scratch_shapes=list(scratch),
        compiler_params=pltpu.CompilerParams(vmem_limit_bytes=VMEM_LIMIT),
    )(*args)


def dot_nn(a, b):
    return jnp.dot(a, b, preferred_element_type=F32)


def dot_nt(a, b):
    return lax.dot_general(a, b, (((1,), (1,)), ((), ())), preferred_element_type=F32)


def dot_tn(a, b):
    return lax.dot_general(a, b, (((0,), (0,)), ((), ())), preferred_element_type=F32)


def flat(x):
    return x.reshape(-1, x.shape[-1])


def run_copies(pairs, sems):
    copies = [pltpu.make_async_copy(src, dst, sems.at[i]) for i, (src, dst) in enumerate(pairs)]
    for copy in copies:
        copy.start()
    return copies


def start_kernel(core_ref, x_ref, c_ref, up_in, down_in, out_ref, up_out, down_out, token, sems):
    del core_ref
    pairs = [(x_ref, token.at[0]), (c_ref, token.at[1]), (up_in, up_out), (down_in, down_out)]
    copies = run_copies(pairs, sems)
    copies[0].wait()
    copies[1].wait()
    for i in range(out_ref.shape[0]):
        out_ref[i] = token[...]
    copies[2].wait()
    copies[3].wait()


def partial_up(g_ref, which, up_ref, down_ref, out_ref):
    half = g_ref.shape[0] // 2
    rows = g_ref[pl.ds(which * half, half)]
    shape = (out_ref.shape[0],) + out_ref.shape[2:]
    out_ref[:, 0] = dot_nn(flat(rows[:, 0]), up_ref[...]).astype(out_ref.dtype).reshape(shape)
    out_ref[:, 1] = dot_nt(flat(rows[:, 1]), down_ref[...]).astype(out_ref.dtype).reshape(shape)


def up_other_kernel(core_ref, g_ref, up_ref, down_ref, out_ref):
    partial_up(g_ref, 1 - core_ref[0], up_ref, down_ref, out_ref)


def up_own_kernel(core_ref, g_ref, up_ref, down_ref, out_ref, x_ref, c_ref):
    partial_up(g_ref, core_ref[0], up_ref, down_ref, out_ref)
    x_ref[...] = flat(g_ref[:, 0]).T
    c_ref[...] = flat(g_ref[:, 1]).T


def add_kernel(a_ref, b_ref, out_ref):
    out_ref[...] = (a_ref[...] + b_ref[...].astype(F32)).astype(BF16)


def middle_kernel(x_ref, out_ref):
    total = jnp.sum(x_ref[...].astype(F32), axis=0)
    hidden, act_grad = total[0], total[1]
    cdf = 0.5 * (1.0 + lax.erf(hidden * 0.7071067811865476))
    slope = cdf + hidden * jnp.exp(-0.5 * hidden * hidden) * 0.3989422804014327
    activated = (hidden * cdf).astype(BF16)
    hid_grad = (act_grad * slope).astype(BF16)
    for i in range(out_ref.shape[0]):
        out_ref[i, 0] = activated
        out_ref[i, 1] = hid_grad


def partial_down(h_ref, up_ref, down_ref, out_ref):
    shape = (out_ref.shape[0],) + out_ref.shape[2:]
    out_ref[:, 0] = dot_nn(flat(h_ref[:, 0]), down_ref[...]).astype(BF16).reshape(shape)
    out_ref[:, 1] = dot_nt(flat(h_ref[:, 1]), up_ref[...]).astype(BF16).reshape(shape)


def down_own_kernel(h_ref, up_ref, down_ref, out_ref):
    partial_down(h_ref, up_ref, down_ref, out_ref)


def down_other_kernel(core_ref, h_ref, own_ref, up_ref, down_ref, out_ref, mine, sems):
    half = own_ref.shape[0]
    core = core_ref[0]
    first = pltpu.make_async_copy(own_ref, out_ref.at[pl.ds(core * half, half)], sems.at[0])
    first.start()
    partial_down(h_ref, up_ref, down_ref, mine)
    second = pltpu.make_async_copy(mine, out_ref.at[pl.ds((1 - core) * half, half)], sems.at[1])
    second.start()
    first.wait()
    second.wait()


def grad_kernel(core_ref, x_ref, c_ref, own_ref, other_ref, up_ref, down_ref):
    half = x_ref.shape[1] // 2
    core = core_ref[0]
    up, down = 0.0, 0.0
    for ref, which in ((own_ref, core), (other_ref, 1 - core)):
        cols = pl.ds(pl.multiple_of(which * half, half), half)
        up = up + dot_nn(x_ref[:, cols], flat(ref[:, 1]))
        down = down + dot_nn(c_ref[:, cols], flat(ref[:, 0]))
    up_ref[...] = up.astype(BF16)
    down_ref[...] = down.astype(BF16).T


def sum_kernel(x_ref, result_ref, in_grad_ref):
    total = jnp.sum(x_ref[...].astype(F32), axis=0)
    result_ref[...] = total[0].astype(BF16)
    in_grad_ref[...] = total[1].astype(BF16)


def exchange(x, axes, first):
    n = x.shape[0]
    order = [(i + first) % n for i in range(n)]
    return lax.all_to_all(x, axes, 0, 0, axis_index_groups=[order], tiled=True)


def on_device(inputs, w_up, w_down, out_grad):
    n_col, n_chips = 16, 16
    tok, model = inputs.shape
    feats = w_up.shape[1]
    half = n_col // 2
    sub = half * tok // n_chips
    core = lax.axis_index("core").astype(jnp.int32).reshape(1)
    hid = (n_chips, 2, sub, feats)
    io = (n_col, 2, tok, model)
    half_io = (half, 2, tok, model)
    turned = (model, n_col * tok)
    weights = [(w_up.shape, BF16), (w_down.shape, BF16)]
    dma = pltpu.SemaphoreType.DMA

    spread, up, down = call(
        start_kernel,
        [(io, BF16)] + weights,
        "shhhhvvv",
        core,
        inputs,
        out_grad,
        w_up,
        w_down,
        scratch=[pltpu.VMEM(io[1:], BF16), dma((4,))],
    )
    g = exchange(spread, COL, COL_FIRST)
    (sent,) = call(up_other_kernel, [(hid, BF16)], "svvvv", core, g, up, down)
    got = lax.ppermute(sent, "core", SWAP)
    kept, x_t, c_t = call(
        up_own_kernel, [(hid, F32), (turned, BF16), (turned, BF16)], "svvvvvv", core, g, up, down
    )
    (part,) = call(add_kernel, [(hid, BF16)], "vvv", kept, got)
    part = exchange(part, CHIPS, CHIPS_FIRST)
    (mine,) = call(middle_kernel, [(hid, BF16)], "vv", part)
    own = exchange(mine, CHIPS, CHIPS_FIRST)
    other = lax.ppermute(own, "core", SWAP)
    (own_out,) = call(down_own_kernel, [(half_io, BF16)], "vvvv", own, w_up, w_down)
    (outs,) = call(
        down_other_kernel,
        [(io, BF16)],
        "svvvvh",
        core,
        other,
        own_out,
        w_up,
        w_down,
        scratch=[pltpu.VMEM(half_io, BF16), dma((2,))],
    )
    outs = exchange(outs, COL, COL_FIRST)
    up_grad, down_grad = call(grad_kernel, weights, "svvvvoo", core, x_t, c_t, own, other)
    up_grad, down_grad, outs = lax.optimization_barrier((up_grad, down_grad, outs))
    result, in_grad = call(sum_kernel, [(inputs.shape, BF16)] * 2, "voo", outs)
    return (result, in_grad, up_grad, down_grad)


def solution(mesh):
    fine = Mesh(mesh.devices.reshape(SIZES), FINE)
    return jax.shard_map(
        on_device,
        mesh=fine,
        in_specs=(P(COL, ROW), P(ROW, COL), P(COL, ROW), P(COL, ROW)),
        out_specs=(P(COL, ROW), P(COL, ROW), P(ROW, COL), P(COL, ROW)),
        check_vma=False,
    )
```

```python
import functools

import jax
import jax.numpy as jnp
from jax import lax
from jax.experimental import pallas as pl
from jax.experimental.pallas import tpu as pltpu
from jax.sharding import Mesh
from jax.sharding import PartitionSpec as P

FINE = ("x_hi", "z", "core", "y", "x_lo")
SIZES = (2, 8, 2, 8, 2)
ROW = ("x_hi", "z", "core")
CHIPS = ("x_hi", "z")
COL = ("y", "x_lo")
SWAP = [(0, 1), (1, 0)]
COL_FIRST = 11
CHIPS_FIRST = 15
BF16 = jnp.bfloat16
F32 = jnp.float32
VMEM_LIMIT = 16 * 1024 * 1024


def call(kernel, outs, spaces, *args, scratch=()):
    kinds = {"s": pltpu.SMEM, "v": pltpu.VMEM, "h": pltpu.HBM, "o": pltpu.VMEM}
    ins, places = spaces[: len(args)], spaces[len(args) :]
    args = [a if s == "s" else pltpu.with_memory_space_constraint(a, kinds[s]) for a, s in zip(args, ins)]
    return pl.pallas_call(
        kernel,
        out_shape=[(jax.ShapeDtypeStruct if s == "o" else kinds[s])(*out) for s, out in zip(places, outs)],
        in_specs=[pl.BlockSpec(memory_space=kinds[s]) for s in ins],
        out_specs=[pl.BlockSpec(memory_space=kinds[s]) for s in places],
        scratch_shapes=list(scratch),
        compiler_params=pltpu.CompilerParams(vmem_limit_bytes=VMEM_LIMIT),
    )(*args)


def dot_nn(a, b):
    return jnp.dot(a, b, preferred_element_type=F32)


def dot_nt(a, b):
    return lax.dot_general(a, b, (((1,), (1,)), ((), ())), preferred_element_type=F32)


def dot_tn(a, b):
    return lax.dot_general(a, b, (((0,), (0,)), ((), ())), preferred_element_type=F32)


def flat(x):
    return x.reshape(-1, x.shape[-1])


def run_copies(pairs, sems):
    copies = [pltpu.make_async_copy(src, dst, sems.at[i]) for i, (src, dst) in enumerate(pairs)]
    for copy in copies:
        copy.start()
    return copies


def start_kernel(core_ref, x_ref, c_ref, up_in, down_in, out_ref, up_out, down_out, token, sems):
    del core_ref
    pairs = [(x_ref, token.at[0]), (c_ref, token.at[1]), (up_in, up_out), (down_in, down_out)]
    copies = run_copies(pairs, sems)
    copies[0].wait()
    copies[1].wait()
    for i in range(out_ref.shape[0]):
        out_ref[i] = token[...]
    copies[2].wait()
    copies[3].wait()


def partial_up(g_ref, which, up_ref, down_ref, out_ref):
    half = g_ref.shape[0] // 2
    rows = g_ref[pl.ds(which * half, half)]
    shape = (out_ref.shape[0],) + out_ref.shape[2:]
    out_ref[:, 0] = dot_nn(flat(rows[:, 0]), up_ref[...]).astype(out_ref.dtype).reshape(shape)
    out_ref[:, 1] = dot_nt(flat(rows[:, 1]), down_ref[...]).astype(out_ref.dtype).reshape(shape)


def up_other_kernel(core_ref, g_ref, up_ref, down_ref, out_ref):
    partial_up(g_ref, 1 - core_ref[0], up_ref, down_ref, out_ref)


def up_own_kernel(core_ref, g_ref, up_ref, down_ref, out_ref, x_ref, c_ref):
    partial_up(g_ref, core_ref[0], up_ref, down_ref, out_ref)
    x_ref[...] = flat(g_ref[:, 0]).T
    c_ref[...] = flat(g_ref[:, 1]).T


def add_kernel(a_ref, b_ref, out_ref):
    out_ref[...] = (a_ref[...] + b_ref[...].astype(F32)).astype(BF16)


def middle_kernel(x_ref, out_ref):
    total = jnp.sum(x_ref[...].astype(F32), axis=0)
    hidden, act_grad = total[0], total[1]
    cdf = 0.5 * (1.0 + lax.erf(hidden * 0.7071067811865476))
    slope = cdf + hidden * jnp.exp(-0.5 * hidden * hidden) * 0.3989422804014327
    activated = (hidden * cdf).astype(BF16)
    hid_grad = (act_grad * slope).astype(BF16)
    for i in range(out_ref.shape[0]):
        out_ref[i, 0] = activated
        out_ref[i, 1] = hid_grad


def partial_down(h_ref, up_ref, down_ref, out_ref):
    shape = (out_ref.shape[0],) + out_ref.shape[2:]
    out_ref[:, 0] = dot_nn(flat(h_ref[:, 0]), down_ref[...]).astype(BF16).reshape(shape)
    out_ref[:, 1] = dot_nt(flat(h_ref[:, 1]), up_ref[...]).astype(BF16).reshape(shape)


def down_own_kernel(h_ref, up_ref, down_ref, out_ref):
    partial_down(h_ref, up_ref, down_ref, out_ref)


def down_other_kernel(core_ref, h_ref, own_ref, up_ref, down_ref, out_ref, mine, sems):
    half = own_ref.shape[0]
    core = core_ref[0]
    first = pltpu.make_async_copy(own_ref, out_ref.at[pl.ds(core * half, half)], sems.at[0])
    first.start()
    partial_down(h_ref, up_ref, down_ref, mine)
    second = pltpu.make_async_copy(mine, out_ref.at[pl.ds((1 - core) * half, half)], sems.at[1])
    second.start()
    first.wait()
    second.wait()


def grad_kernel(core_ref, x_ref, c_ref, own_ref, other_ref, up_ref, down_ref):
    half = x_ref.shape[1] // 2
    core = core_ref[0]
    up, down = 0.0, 0.0
    for ref, which in ((own_ref, core), (other_ref, 1 - core)):
        cols = pl.ds(pl.multiple_of(which * half, half), half)
        up = up + dot_nn(x_ref[:, cols], flat(ref[:, 1]))
        down = down + dot_nn(c_ref[:, cols], flat(ref[:, 0]))
    up_ref[...] = up.astype(BF16)
    down_ref[...] = down.astype(BF16).T


def sum_kernel(x_ref, result_ref, in_grad_ref):
    total = jnp.sum(x_ref[...].astype(F32), axis=0)
    result_ref[...] = total[0].astype(BF16)
    in_grad_ref[...] = total[1].astype(BF16)


def exchange(x, axes, first):
    n = x.shape[0]
    order = [(i + first) % n for i in range(n)]
    return lax.all_to_all(x, axes, 0, 0, axis_index_groups=[order], tiled=True)


def on_device(inputs, w_up, w_down, out_grad):
    n_col, n_chips = 16, 16
    tok, model = inputs.shape
    feats = w_up.shape[1]
    half = n_col // 2
    sub = half * tok // n_chips
    core = lax.axis_index("core").astype(jnp.int32).reshape(1)
    hid = (n_chips, 2, sub, feats)
    io = (n_col, 2, tok, model)
    half_io = (half, 2, tok, model)
    turned = (model, n_col * tok)
    weights = [(w_up.shape, BF16), (w_down.shape, BF16)]
    dma = pltpu.SemaphoreType.DMA

    spread, up, down = call(
        start_kernel,
        [(io, BF16)] + weights,
        "shhhhvvv",
        core,
        inputs,
        out_grad,
        w_up,
        w_down,
        scratch=[pltpu.VMEM(io[1:], BF16), dma((4,))],
    )
    g = exchange(spread, COL, COL_FIRST)
    (sent,) = call(up_other_kernel, [(hid, BF16)], "svvvv", core, g, up, down)
    got = lax.ppermute(sent, "core", SWAP)
    kept, x_t, c_t = call(
        up_own_kernel, [(hid, F32), (turned, BF16), (turned, BF16)], "svvvvvv", core, g, up, down
    )
    (part,) = call(add_kernel, [(hid, BF16)], "vvv", kept, got)
    part = exchange(part, CHIPS, CHIPS_FIRST)
    (mine,) = call(middle_kernel, [(hid, BF16)], "vv", part)
    own = exchange(mine, CHIPS, CHIPS_FIRST)
    other = lax.ppermute(own, "core", SWAP)
    (own_out,) = call(down_own_kernel, [(half_io, BF16)], "vvvv", own, w_up, w_down)
    (outs,) = call(
        down_other_kernel,
        [(io, BF16)],
        "svvvvh",
        core,
        other,
        own_out,
        w_up,
        w_down,
        scratch=[pltpu.VMEM(half_io, BF16), dma((2,))],
    )
    outs = exchange(outs, COL, COL_FIRST)
    up_grad, down_grad = call(grad_kernel, weights, "svvvvoo", core, x_t, c_t, own, other)
    up_grad, down_grad, outs = lax.optimization_barrier((up_grad, down_grad, outs))
    result, in_grad = call(sum_kernel, [(inputs.shape, BF16)] * 2, "voo", outs)
    return (result, in_grad, up_grad, down_grad)


def solution(mesh):
    fine = Mesh(mesh.devices.reshape(SIZES), FINE)
    return jax.shard_map(
        on_device,
        mesh=fine,
        in_specs=(P(COL, ROW), P(ROW, COL), P(COL, ROW), P(COL, ROW)),
        out_specs=(P(COL, ROW), P(COL, ROW), P(ROW, COL), P(COL, ROW)),
        check_vma=False,
    )
```

```python
import functools

import jax
import jax.numpy as jnp
from jax import lax
from jax.experimental import pallas as pl
from jax.experimental.pallas import tpu as pltpu
from jax.sharding import Mesh
from jax.sharding import PartitionSpec as P

FINE = ("x_hi", "z", "core", "y", "x_lo")
SIZES = (2, 8, 2, 8, 2)
ROW = ("x_hi", "z", "core")
CHIPS = ("x_hi", "z")
COL = ("y", "x_lo")
SWAP = [(0, 1), (1, 0)]
COL_FIRST = 11
CHIPS_FIRST = 15
BF16 = jnp.bfloat16
F32 = jnp.float32
VMEM_LIMIT = 16 * 1024 * 1024


def call(kernel, outs, spaces, *args, scratch=()):
    kinds = {"s": pltpu.SMEM, "v": pltpu.VMEM, "h": pltpu.HBM, "o": pltpu.VMEM}
    ins, places = spaces[: len(args)], spaces[len(args) :]
    args = [a if s == "s" else pltpu.with_memory_space_constraint(a, kinds[s]) for a, s in zip(args, ins)]
    return pl.pallas_call(
        kernel,
        out_shape=[(jax.ShapeDtypeStruct if s == "o" else kinds[s])(*out) for s, out in zip(places, outs)],
        in_specs=[pl.BlockSpec(memory_space=kinds[s]) for s in ins],
        out_specs=[pl.BlockSpec(memory_space=kinds[s]) for s in places],
        scratch_shapes=list(scratch),
        compiler_params=pltpu.CompilerParams(vmem_limit_bytes=VMEM_LIMIT),
    )(*args)


def dot_nn(a, b):
    return jnp.dot(a, b, preferred_element_type=F32)


def dot_nt(a, b):
    return lax.dot_general(a, b, (((1,), (1,)), ((), ())), preferred_element_type=F32)


def dot_tn(a, b):
    return lax.dot_general(a, b, (((0,), (0,)), ((), ())), preferred_element_type=F32)


def flat(x):
    return x.reshape(-1, x.shape[-1])


def run_copies(pairs, sems):
    copies = [pltpu.make_async_copy(src, dst, sems.at[i]) for i, (src, dst) in enumerate(pairs)]
    for copy in copies:
        copy.start()
    return copies


def start_kernel(core_ref, x_ref, c_ref, up_in, down_in, out_ref, up_out, down_out, token, sems):
    del core_ref
    pairs = [(x_ref, token.at[0]), (c_ref, token.at[1]), (up_in, up_out), (down_in, down_out)]
    copies = run_copies(pairs, sems)
    copies[0].wait()
    copies[1].wait()
    for i in range(out_ref.shape[0]):
        out_ref[i] = token[...]
    copies[2].wait()
    copies[3].wait()


def partial_up(g_ref, which, up_ref, down_ref, out_ref):
    half = g_ref.shape[0] // 2
    rows = g_ref[pl.ds(which * half, half)]
    shape = (out_ref.shape[0],) + out_ref.shape[2:]
    out_ref[:, 0] = dot_nn(flat(rows[:, 0]), up_ref[...]).astype(out_ref.dtype).reshape(shape)
    out_ref[:, 1] = dot_nt(flat(rows[:, 1]), down_ref[...]).astype(out_ref.dtype).reshape(shape)


def up_other_kernel(core_ref, g_ref, up_ref, down_ref, out_ref):
    partial_up(g_ref, 1 - core_ref[0], up_ref, down_ref, out_ref)


def up_own_kernel(core_ref, g_ref, up_ref, down_ref, out_ref, x_ref, c_ref):
    partial_up(g_ref, core_ref[0], up_ref, down_ref, out_ref)
    x_ref[...] = flat(g_ref[:, 0]).T
    c_ref[...] = flat(g_ref[:, 1]).T


def add_kernel(a_ref, b_ref, out_ref):
    out_ref[...] = (a_ref[...] + b_ref[...].astype(F32)).astype(BF16)


def middle_kernel(x_ref, out_ref):
    total = jnp.sum(x_ref[...].astype(F32), axis=0)
    hidden, act_grad = total[0], total[1]
    cdf = 0.5 * (1.0 + lax.erf(hidden * 0.7071067811865476))
    slope = cdf + hidden * jnp.exp(-0.5 * hidden * hidden) * 0.3989422804014327
    activated = (hidden * cdf).astype(BF16)
    hid_grad = (act_grad * slope).astype(BF16)
    for i in range(out_ref.shape[0]):
        out_ref[i, 0] = activated
        out_ref[i, 1] = hid_grad


def partial_down(h_ref, up_ref, down_ref, out_ref):
    shape = (out_ref.shape[0],) + out_ref.shape[2:]
    out_ref[:, 0] = dot_nn(flat(h_ref[:, 0]), down_ref[...]).astype(BF16).reshape(shape)
    out_ref[:, 1] = dot_nt(flat(h_ref[:, 1]), up_ref[...]).astype(BF16).reshape(shape)


def down_own_kernel(h_ref, up_ref, down_ref, out_ref):
    partial_down(h_ref, up_ref, down_ref, out_ref)


def down_other_kernel(core_ref, h_ref, own_ref, up_ref, down_ref, out_ref, mine, sems):
    half = own_ref.shape[0]
    core = core_ref[0]
    first = pltpu.make_async_copy(own_ref, out_ref.at[pl.ds(core * half, half)], sems.at[0])
    first.start()
    partial_down(h_ref, up_ref, down_ref, mine)
    second = pltpu.make_async_copy(mine, out_ref.at[pl.ds((1 - core) * half, half)], sems.at[1])
    second.start()
    first.wait()
    second.wait()


def grad_kernel(core_ref, x_ref, c_ref, own_ref, other_ref, up_ref, down_ref, up, down, sems):
    half = x_ref.shape[1] // 2
    core = core_ref[0]
    own = pl.ds(pl.multiple_of(core * half, half), half)
    other = pl.ds(pl.multiple_of((1 - core) * half, half), half)

    def product(turned, which):
        total = dot_nn(turned[:, own], flat(own_ref[:, which])) + dot_nn(turned[:, other], flat(other_ref[:, which]))
        return total.astype(BF16)

    up[...] = product(x_ref, 1)
    first = pltpu.make_async_copy(up, up_ref, sems.at[0])
    first.start()
    down[...] = product(c_ref, 0).T
    second = pltpu.make_async_copy(down, down_ref, sems.at[1])
    second.start()
    first.wait()
    second.wait()


def sum_kernel(x_ref, result_ref, in_grad_ref):
    total = jnp.sum(x_ref[...].astype(F32), axis=0)
    result_ref[...] = total[0].astype(BF16)
    in_grad_ref[...] = total[1].astype(BF16)


def exchange(x, axes, first):
    n = x.shape[0]
    order = [(i + first) % n for i in range(n)]
    return lax.all_to_all(x, axes, 0, 0, axis_index_groups=[order], tiled=True)


def on_device(inputs, w_up, w_down, out_grad):
    n_col, n_chips = 16, 16
    tok, model = inputs.shape
    feats = w_up.shape[1]
    half = n_col // 2
    sub = half * tok // n_chips
    core = lax.axis_index("core").astype(jnp.int32).reshape(1)
    hid = (n_chips, 2, sub, feats)
    io = (n_col, 2, tok, model)
    half_io = (half, 2, tok, model)
    turned = (model, n_col * tok)
    weights = [(w_up.shape, BF16), (w_down.shape, BF16)]
    dma = pltpu.SemaphoreType.DMA

    spread, up, down = call(
        start_kernel,
        [(io, BF16)] + weights,
        "shhhhvvv",
        core,
        inputs,
        out_grad,
        w_up,
        w_down,
        scratch=[pltpu.VMEM(io[1:], BF16), dma((4,))],
    )
    g = exchange(spread, COL, COL_FIRST)
    (sent,) = call(up_other_kernel, [(hid, BF16)], "svvvv", core, g, up, down)
    got = lax.ppermute(sent, "core", SWAP)
    kept, x_t, c_t = call(
        up_own_kernel, [(hid, F32), (turned, BF16), (turned, BF16)], "svvvvvv", core, g, up, down
    )
    (part,) = call(add_kernel, [(hid, BF16)], "vvv", kept, got)
    part = exchange(part, CHIPS, CHIPS_FIRST)
    (mine,) = call(middle_kernel, [(hid, BF16)], "vv", part)
    own = exchange(mine, CHIPS, CHIPS_FIRST)
    other = lax.ppermute(own, "core", SWAP)
    (own_out,) = call(down_own_kernel, [(half_io, BF16)], "vvvv", own, w_up, w_down)
    (outs,) = call(
        down_other_kernel,
        [(io, BF16)],
        "svvvvh",
        core,
        other,
        own_out,
        w_up,
        w_down,
        scratch=[pltpu.VMEM(half_io, BF16), dma((2,))],
    )
    outs = exchange(outs, COL, COL_FIRST)
    up_grad, down_grad = call(
        grad_kernel,
        weights,
        "svvvvhh",
        core,
        x_t,
        c_t,
        own,
        other,
        scratch=[pltpu.VMEM(w_up.shape, BF16), pltpu.VMEM(w_down.shape, BF16), dma((2,))],
    )
    up_grad, down_grad, outs = lax.optimization_barrier((up_grad, down_grad, outs))
    result, in_grad = call(sum_kernel, [(inputs.shape, BF16)] * 2, "voo", outs)
    return (result, in_grad, up_grad, down_grad)


def solution(mesh):
    fine = Mesh(mesh.devices.reshape(SIZES), FINE)
    return jax.shard_map(
        on_device,
        mesh=fine,
        in_specs=(P(COL, ROW), P(ROW, COL), P(COL, ROW), P(COL, ROW)),
        out_specs=(P(COL, ROW), P(COL, ROW), P(ROW, COL), P(COL, ROW)),
        check_vma=False,
    )
```
